32 devices in a mesh: seq: 16 (over z, y, x), col: 2 (over core).
Axes of the slice: x: 2, y: 2, z: 4, core: 2. Of those that a mesh axis runs over, the one named last changes fastest.
Arguments:
- hidden: bfloat16 [4, 96, 2304], P(None, None, 'seq'), may hold values from -6 to 6
- key_cache: bfloat16 [1152, 128, 2048], P('seq', None, 'col'), may hold values from -300 to 300
- value_cache: bfloat16 [1152, 128, 2048], P('seq', None, 'col'), may hold values from -6 to 6
- page_table: int32 [96, 128], replicated, may hold values from 0 to 1151, as said below
- cache_len: int32 [96], replicated, may hold values from 1 to 16380, as said below
- order: int32 [96], replicated, may hold values from 0 to 95, each once
- route_ids: int32 [4, 96, 2], replicated, may hold values from 0 to 7, all different within a row; in each aligned block of 96 rows (0 to 95, 96 to 191, ..., all dimensions but the last counted through in order) at most 48 rows name the same one
- w_qkv: bfloat16 [2304, 3, 2048], P('seq', None, 'col'), may hold values from -0.125 to 0.125
- w_out: bfloat16 [2048, 2304], P('col', 'seq'), may hold values from -0.125 to 0.125
- w_router: bfloat16 [2304, 8], replicated, may hold values from -0.125 to 0.125
- w_gate_up: bfloat16 [8, 2304, 2, 5760], P('col', None, None, 'seq'), may hold values from -0.125 to 0.125
- w_down: bfloat16 [8, 5760, 2304], P('col', 'seq'), may hold values from -0.109375 to 0.109375
Outputs:
- layer_out: bfloat16 [4, 96, 2304], P(None, None, 'seq')
- new_keys: bfloat16 [4, 96, 2048], P(None, None, 'col')
- new_values: bfloat16 [4, 96, 2048], P(None, None, 'col')
The draws below stay inside these ranges and needn't reach their ends.
Inputs may be any that keep to these rules, and one draw needn't show every extreme that they name: `cache_len`: one request's cache holds exactly 16380 tokens; 4 requests hold more than 640 tokens, the others at most 640. `page_table`: for request r the entries 0 to ceil((cache_len[r] + 4) / 128) - 1 name pages that no other such entry names; later entries are never read. `order`: each request sits in exactly one batch slot. `route_ids`: the two experts of a row differ; in each step no expert is named by more than 48 requests.
All inputs are finite; a program needn't handle non-finite values.
Results may differ from the reference program's by a relative error of at most 0.011.
Values may be sent and summed in bfloat16 or wider, within the bound.
A program may use at most 256 MiB of HBM per device.

```python
import math
import jax
import jax.numpy as jnp
import numpy as np
from jax import lax

D = 2304
HEADS = 32
HEAD_DIM = 64
EXPERTS = 8
FF = 5760
PAGE = 128
MAXP = 128
STEPS = 4
REQS = 96
PAGES = 1152
CAP = 48


def layout(key):
    base_key = jax.random.fold_in(key, 7)
    key_long, key_short, key_rank, key_pool, key_filler = jax.random.split(base_key, 5)
    longest = MAXP * PAGE - STEPS
    long_count = max(1, REQS // 24)
    short_len = jax.random.randint(key_short, (REQS,), 1, 5 * PAGE + 1)
    long_len = jax.random.randint(key_long, (REQS,), 5 * PAGE + 1, longest + 1)
    ranking = jax.random.permutation(key_rank, REQS)
    lengths = jnp.where(ranking < long_count, long_len, short_len)
    lengths = jnp.where(ranking == 0, longest, lengths)
    needed = (lengths + STEPS + PAGE - 1) // PAGE
    offsets = jnp.cumsum(needed) - needed
    page_pool = jax.random.permutation(key_pool, PAGES)
    columns = jnp.arange(MAXP)
    spots = jnp.minimum(offsets[:, None] + columns[None, :], PAGES - 1)
    filler = jax.random.randint(key_filler, (REQS, MAXP), 0, PAGES)
    table = jnp.where(columns[None, :] < needed[:, None], page_pool[spots], filler)
    return (lengths.astype(jnp.int32), table.astype(jnp.int32))


def draw_cache_len(key, part):
    return layout(key)[0]


def draw_page_table(key, part):
    return layout(key)[1]


def draw_key_cache(key, part):
    key_base = jax.random.fold_in(jax.random.fold_in(key, 11), 0)
    shape = (PAGES, PAGE, HEADS * HEAD_DIM)
    return jax.random.normal(key_base, shape, jnp.float32).astype(jnp.bfloat16)


def spiked(entries, key, source, target, shards_of, factor):
    owner, partner = [(jnp.arange(entries.shape[dim]) // (entries.shape[dim] // shards_of)).reshape([-1 if axis == dim else 1 for axis in range(entries.ndim)]) for dim in (source, target)]
    chosen = jax.random.permutation(key, shards_of)[partner]
    strong = (owner == chosen) | (owner == (partner + shards_of // 2) % shards_of)
    return jnp.where(strong, factor * entries, entries)


def level_of(key, dims, cuts, least, top_value):
    def one(axis_at, shards_of):
        heights = jax.random.uniform(jax.random.fold_in(jax.random.fold_in(key, 6), axis_at), (shards_of,), jnp.float32, least / len(cuts), top_value / len(cuts))
        return jnp.repeat(jnp.exp(heights), dims[axis_at] // shards_of).reshape((-1,) + (1,) * (len(dims) - axis_at - 1))

    factor_of = one(*cuts[0])
    for cut in cuts[1:]:
        factor_of = factor_of * one(*cut)
    return factor_of


def shared_out(stream_key, own, number, rows, amount, top, reach, skew):
    order = jax.random.permutation(stream_key, amount)
    crowded, usual = shares(amount, rows * top, reach, skew, True), shares(amount, rows * top, reach, skew, False)
    places = jnp.arange(amount)

    def named(tallies, turn):
        used = int((tallies > 0).sum())
        fixed = max(1, used // 4)
        passed = fixed + (places - fixed + turn * (used - fixed)) % max(1, amount - fixed)
        return jnp.zeros((amount,), jnp.int32).at[order[jnp.where(places < fixed, places, passed)]].set(jnp.asarray(tallies, jnp.int32))

    tallies = jnp.where(number % 4 == 0, named(crowded, number // 4), named(usual, number - number // 4 - 1))
    mixed = jax.random.permutation(jax.random.fold_in(own, 3), amount)
    giver, taker = mixed[0:amount // 2 * 2:2], mixed[1:amount // 2 * 2:2]
    slack = jnp.minimum(tallies[giver] - 1, reach - tallies[taker]) // 2
    slack = jnp.where((giver == order[0]) | (taker == order[0]) | (tallies[taker] == 0), 0, jnp.maximum(slack, 0))
    passed = jax.random.randint(jax.random.fold_in(own, 4), (amount // 2,), 0, 1 << 20) % (slack + 1)
    tallies = tallies.at[giver].add(-passed).at[taker].add(passed)
    labels = jnp.searchsorted(jnp.cumsum(tallies), jnp.arange(rows * top), side="right").astype(jnp.int32)
    grid = labels.reshape(top, rows).T
    grid = grid[jax.random.permutation(jax.random.fold_in(own, 1), rows)]
    turn = jax.random.randint(jax.random.fold_in(own, 2), (rows, 1), 0, top)
    return jnp.take_along_axis(grid, (jnp.arange(top)[None, :] + turn) % top, axis=1)


def shares(number_of, total, limit, slope, full):
    weights = [(1 << 20) // math.isqrt(grade ** slope) + 1 for grade in range(1, number_of + 1)]
    largest = limit if full else min(limit, max(-(-total // number_of), total * weights[0] // sum(weights)))
    least = 1 if total - largest >= number_of - 1 else 0
    given, spare = [largest] + [least] * (number_of - 1), total - largest - least * (number_of - 1)
    while spare > 0:
        movable = [i for i in range(1, number_of) if given[i] < largest] or [i for i in range(1, number_of) if given[i] < limit]
        pool, left = sum([weights[i] for i in movable]), spare
        for i in movable:
            more = min(limit - given[i], max(1, left * weights[i] // pool), spare)
            given[i] = given[i] + more
            spare = spare - more
    return np.array(given)


def noise(key, dims, deviation, bound, shards=(), kind=jnp.bfloat16):
    loudness = level_of(key, dims, shards, -0.22, 0.18) if shards else 1.0
    result = jax.random.normal(key, dims, jnp.float32) * deviation * loudness
    return jnp.minimum(jnp.maximum(result, -bound), bound).astype(kind)


def heavy_noise(rng, dims, width, limit, pieces, heavy, kind=jnp.bfloat16):
    result = width * jax.random.normal(rng, dims, jnp.float32)
    if pieces:
        result = result * level_of(rng, dims, pieces, -0.22, 0.18)
    return jnp.clip(spiked(result, jax.random.fold_in(rng, 3), *heavy), -limit, limit).astype(kind)


def setup_inputs(seed: int = 0) -> dict:
    splits = jax.random.split(jax.random.key(seed), 13)
    hidden = noise(splits[0], (STEPS, REQS, D), 1.0, 6.0, ((2, 16),))
    key_cache = draw_key_cache(jax.random.fold_in(splits[12], 71), 0)
    value_cache = noise(splits[2], (PAGES, PAGE, HEADS * HEAD_DIM), 1.0, 6.0, ((0, 16), (2, 2)))
    page_table = draw_page_table(jax.random.fold_in(splits[12], 71), 0)
    cache_len = draw_cache_len(jax.random.fold_in(splits[12], 71), 0)
    order = jax.random.permutation(splits[5], REQS).astype(jnp.int32)
    route_ids_keys = jax.random.split(jax.random.fold_in(splits[6], 1), STEPS * REQS // REQS)
    route_ids_turns = jax.random.permutation(jax.random.fold_in(splits[6], 3), STEPS * REQS // REQS)
    route_ids = jax.vmap(lambda own, number: shared_out(jax.random.fold_in(splits[6], 2), own, number, REQS, EXPERTS, 2, CAP, 2))(route_ids_keys, route_ids_turns).reshape((STEPS, REQS, 2))
    w_qkv = noise(splits[7], (D, 3, HEADS * HEAD_DIM), D ** -0.5, 0.125, ((0, 16), (2, 2)))
    w_out = noise(splits[8], (HEADS * HEAD_DIM, D), (HEADS * HEAD_DIM) ** -0.5, 0.125, ((0, 2), (1, 16)))
    w_router = noise(splits[9], (D, EXPERTS), D ** -0.5, 0.125)
    w_gate_up = noise(splits[10], (EXPERTS, D, 2, FF), D ** -0.5, 0.125, ((0, 2), (3, 16)))
    w_down = heavy_noise(splits[11], (EXPERTS, FF, D), FF ** -0.5, 0.109375, ((0, 2), (1, 16)), (1, 2, 16, 2.0))
    return dict(hidden=hidden, key_cache=key_cache, value_cache=value_cache, page_table=page_table, cache_len=cache_len, order=order, route_ids=route_ids, w_qkv=w_qkv, w_out=w_out, w_router=w_router, w_gate_up=w_gate_up, w_down=w_down)


EPSILON = 1e-05

def rotate(row_data, positions, head_dim):
    head_count = row_data.shape[1] // head_dim
    half_dim = head_dim // 2
    frequency = jnp.exp(-jnp.log(10000.0) * 2.0 * jnp.arange(half_dim, dtype=jnp.float32) / head_dim)
    angles = positions.astype(jnp.float32)[:, None] * frequency[None, :]
    cosine = jnp.cos(angles)[:, None, :]
    sines = jnp.sin(angles)[:, None, :]
    by_head = row_data.reshape(row_data.shape[0], head_count, head_dim)
    front_half = by_head[:, :, :half_dim]
    back_half = by_head[:, :, half_dim:]
    turned = jnp.concatenate([front_half * cosine - back_half * sines, back_half * cosine + front_half * sines], axis=2)
    return turned.reshape(row_data.shape)

def reference(hidden, key_cache, value_cache, page_table, cache_len, order, route_ids, w_qkv, w_out, w_router, w_gate_up, w_down):
    columns = HEADS * HEAD_DIM
    span = MAXP * PAGE
    w_proj = w_qkv.reshape(D, 3 * columns)
    new_keys = jnp.zeros((STEPS, REQS, columns), jnp.bfloat16)
    new_values = jnp.zeros((STEPS, REQS, columns), jnp.bfloat16)
    expert_ids = jnp.arange(EXPERTS)
    layers = []
    for moment in range(STEPS):
        inputs = jnp.zeros((REQS, D), jnp.bfloat16).at[order].set(hidden[moment])
        wide_in = inputs.astype(jnp.float32)
        inv_one = lax.rsqrt(lax.optimization_barrier(jnp.mean(wide_in * wide_in, axis=1)) + EPSILON)
        proj = jnp.dot(inputs, w_proj, preferred_element_type=jnp.float32) * inv_one[:, None]
        positions = cache_len + moment
        query = rotate(proj[:, :columns], positions, HEAD_DIM).astype(jnp.bfloat16)
        new_keys = new_keys.at[moment].set(rotate(proj[:, columns:2 * columns], positions, HEAD_DIM).astype(jnp.bfloat16))
        new_values = new_values.at[moment].set(proj[:, 2 * columns:].astype(jnp.bfloat16))
        fresh_keys = jnp.transpose(new_keys, (1, 0, 2))
        fresh_values = jnp.transpose(new_values, (1, 0, 2))

        def attend_one(request_args):
            query_row, table_row, length, key_new, value_new = request_args
            key_rows = jnp.concatenate([key_cache[table_row].reshape(span, columns), key_new], axis=0)
            value_rows = jnp.concatenate([value_cache[table_row].reshape(span, columns), value_new], axis=0)
            position_ids = jnp.arange(span + STEPS)
            visible = jnp.where(position_ids < span, position_ids < length, position_ids - span <= moment)
            scores = jnp.einsum('hd,khd->hk', query_row.reshape(HEADS, HEAD_DIM).astype(jnp.float32), key_rows.reshape(span + STEPS, HEADS, HEAD_DIM).astype(jnp.float32), precision=lax.Precision.HIGHEST) * HEAD_DIM ** (-0.5)
            scores = jnp.where(visible[None, :], scores, -jnp.inf)
            top_score = lax.optimization_barrier(jnp.max(scores, axis=1, keepdims=True))
            weight = jnp.where(visible[None, :], jnp.exp(scores - top_score), 0.0)
            lowered = lax.optimization_barrier(weight.astype(jnp.bfloat16)).astype(jnp.float32)
            summed = jnp.einsum('hk,khd->hd', lowered, value_rows.reshape(span + STEPS, HEADS, HEAD_DIM).astype(jnp.float32), precision=lax.Precision.HIGHEST)
            return (summed / lax.optimization_barrier(jnp.sum(weight, axis=1, keepdims=True))).reshape(columns).astype(jnp.bfloat16)
        attention = lax.map(attend_one, (query, page_table, cache_len, fresh_keys, fresh_values))
        mid = (wide_in + jnp.dot(attention, w_out, preferred_element_type=jnp.float32)).astype(jnp.bfloat16)
        wide_mid = mid.astype(jnp.float32)
        inv_two = lax.rsqrt(lax.optimization_barrier(jnp.mean(wide_mid * wide_mid, axis=1)) + EPSILON)
        logits = jnp.dot(mid, w_router, preferred_element_type=jnp.float32) * inv_two[:, None]
        chosen = route_ids[moment]
        first_pick = chosen[:, 0:1] == expert_ids[None, :]
        second_pick = chosen[:, 1:2] == expert_ids[None, :]
        first_share = jax.nn.sigmoid(lax.optimization_barrier(jnp.sum(jnp.where(first_pick, logits, 0.0), axis=1)) - lax.optimization_barrier(jnp.sum(jnp.where(second_pick, logits, 0.0), axis=1)))
        gate_rows = jnp.where(first_pick, first_share[:, None], 0.0) + jnp.where(second_pick, 1.0 - first_share[:, None], 0.0)
        mixture = wide_mid
        for expert in range(EXPERTS):
            pair_sum = jnp.dot(mid, w_gate_up[expert].reshape(D, 2 * FF), preferred_element_type=jnp.float32) * inv_two[:, None]
            active = (jax.nn.silu(pair_sum[:, :FF]) * pair_sum[:, FF:]).astype(jnp.bfloat16)
            mixture = mixture + gate_rows[:, expert:expert + 1] * jnp.dot(active, w_down[expert], preferred_element_type=jnp.float32)
        layers.append(mixture.astype(jnp.bfloat16))
    return (jnp.stack(layers), new_keys, new_values)
```

```python
import jax
import jax.numpy as jnp
from jax import lax
from jax.experimental import pallas as pl
from jax.experimental.pallas import tpu as pltpu
from jax.sharding import PartitionSpec as P

HEAD_DIM = 64


EPSILON = 1e-05
LOWEST = -1e30


def rotate(row_data, positions, head_dim):
    head_count = row_data.shape[1] // head_dim
    half_dim = head_dim // 2
    frequency = jnp.exp(
        -jnp.log(10000.0) * 2.0 * jnp.arange(half_dim, dtype=jnp.float32) / head_dim
    )
    angles = positions.astype(jnp.float32)[:, None] * frequency[None, :]
    cosine = jnp.cos(angles)[:, None, :]
    sines = jnp.sin(angles)[:, None, :]
    by_head = row_data.reshape(row_data.shape[0], head_count, head_dim)
    front_half = by_head[:, :, :half_dim]
    back_half = by_head[:, :, half_dim:]
    turned = jnp.concatenate(
        [front_half * cosine - back_half * sines, back_half * cosine + front_half * sines], axis=2
    )
    return turned.reshape(row_data.shape)


def attend_kernel(owner_ref, count_ref, q_ref, k_ref, v_ref, sum_ref, peak_ref, total_ref):
    page = pl.program_id(0)
    steps, cols = q_ref.shape[1], q_ref.shape[2]
    size = k_ref.shape[1]
    padded = peak_ref.shape[2] // steps
    count = count_ref[page]
    wide = q_ref[0].astype(jnp.float32)
    own = lax.broadcasted_iota(jnp.int32, (padded, cols), 1) // HEAD_DIM == lax.broadcasted_iota(
        jnp.int32, (padded, cols), 0
    )
    spread = jnp.concatenate(
        [jnp.where(own, wide[n : n + 1, :], 0.0) for n in range(steps)], axis=0
    ).astype(jnp.bfloat16)
    scores = lax.dot_general(
        k_ref[0], spread, (((1,), (1,)), ((), ())), preferred_element_type=jnp.float32
    ) * (HEAD_DIM ** (-0.5))
    live = lax.broadcasted_iota(jnp.int32, (size, steps * padded), 0) < count
    scores = jnp.where(live, scores, LOWEST)
    peak = jnp.max(scores, axis=0, keepdims=True)
    weights = jnp.where(live, jnp.exp(scores - peak), 0.0)
    peak_ref[0] = peak
    total_ref[0] = jnp.sum(weights, axis=0, keepdims=True)
    mixed = lax.dot_general(
        weights.astype(jnp.bfloat16),
        v_ref[0],
        (((0,), (0,)), ((), ())),
        preferred_element_type=jnp.float32,
    )
    for n in range(steps):
        part = jnp.where(own, mixed[n * padded : (n + 1) * padded, :], 0.0)
        sum_ref[0, n : n + 1, :] = jnp.sum(part, axis=0, keepdims=True)


def attend_pages(owner, count, query, keys, values):
    pages, size, cols = keys.shape
    steps = query.shape[1]
    heads = cols // HEAD_DIM
    padded = -(-heads // 8) * 8
    sums, peak, total = pl.pallas_call(
        attend_kernel,
        grid_spec=pltpu.PrefetchScalarGridSpec(
            num_scalar_prefetch=2,
            grid=(pages,),
            in_specs=[
                pl.BlockSpec((1, steps, cols), lambda p, o, c: (o[p], 0, 0)),
                pl.BlockSpec((1, size, cols), lambda p, o, c: (p, 0, 0)),
                pl.BlockSpec((1, size, cols), lambda p, o, c: (p, 0, 0)),
            ],
            out_specs=[
                pl.BlockSpec((1, steps, cols), lambda p, o, c: (p, 0, 0)),
                pl.BlockSpec((1, 1, steps * padded), lambda p, o, c: (p, 0, 0)),
                pl.BlockSpec((1, 1, steps * padded), lambda p, o, c: (p, 0, 0)),
            ],
        ),
        out_shape=(
            jax.ShapeDtypeStruct((pages, steps, cols), jnp.float32),
            jax.ShapeDtypeStruct((pages, 1, steps * padded), jnp.float32),
            jax.ShapeDtypeStruct((pages, 1, steps * padded), jnp.float32),
        ),
        cost_estimate=pl.CostEstimate(
            flops=4 * pages * steps * padded * size * cols,
            bytes_accessed=4 * pages * size * cols,
            transcendentals=pages * steps * padded * size,
        ),
    )(owner, count, query, keys, values)
    peak = peak.reshape(pages, steps, padded)[:, :, :heads]
    total = total.reshape(pages, steps, padded)[:, :, :heads]
    return sums, peak, total


def pieces(value, count):
    out = []
    for _ in range(count):
        part = lax.reduce_precision(value, 8, 7)
        out.append(part.astype(jnp.bfloat16))
        value = value - part
    return out


def exchange(blocks):
    return lax.all_to_all(blocks, "seq", split_axis=0, concat_axis=0, tiled=True)


def col_scatter(rows):
    if lax.axis_size("col") == 2:
        half = rows.shape[0] // 2
        me = lax.axis_index("col")
        mine = lax.dynamic_slice_in_dim(rows, me * half, half, 0)
        theirs = lax.dynamic_slice_in_dim(rows, (1 - me) * half, half, 0)
        return mine + lax.ppermute(theirs, "col", [(0, 1), (1, 0)])
    return lax.psum_scatter(rows, "col", scatter_dimension=0, tiled=True)


def col_gather(rows):
    if lax.axis_size("col") == 2:
        me = lax.axis_index("col")
        other = lax.ppermute(rows, "col", [(0, 1), (1, 0)])
        first = jnp.where(me == 0, rows, other)
        second = jnp.where(me == 0, other, rows)
        return jnp.concatenate([first, second], axis=0)
    return lax.all_gather(rows, "col", axis=0, tiled=True)


def local(
    hidden,
    key_cache,
    value_cache,
    page_table,
    cache_len,
    order,
    route_ids,
    w_qkv,
    w_out,
    w_router,
    w_gate_up,
    w_down,
):
    steps, requests, width_loc = hidden.shape
    pages_loc, page_size, cols = key_cache.shape
    heads = cols // HEAD_DIM
    shards = lax.axis_size("seq")
    width_all = width_loc * shards
    experts_loc = w_gate_up.shape[0]
    ff_loc = w_gate_up.shape[3]
    expert_count = w_router.shape[1]
    expert_base = lax.axis_index("col") * experts_loc
    seq_index = lax.axis_index("seq")
    share = -(-requests // shards)
    filler = share * shards - requests
    row_count = steps * requests
    own_rows = share * steps

    placing = (order[:, None] == jnp.arange(requests)[None, :]).astype(jnp.bfloat16)
    inputs = jnp.einsum("nsc,sr->rnc", hidden, placing, preferred_element_type=jnp.float32).astype(
        jnp.bfloat16
    )
    flat_in = inputs.reshape(row_count, width_loc)
    wide_in = flat_in.astype(jnp.float32)
    squares = jnp.sum(wide_in * wide_in, axis=1, keepdims=True)
    partial = jnp.dot(
        flat_in, w_qkv.reshape(width_loc, 3 * cols), preferred_element_type=jnp.float32
    ).astype(jnp.bfloat16)
    tail = jnp.pad(jnp.concatenate(pieces(squares, 3), axis=1), ((0, 0), (0, 125)))
    sent = jnp.pad(jnp.concatenate([partial, tail], axis=1), ((0, filler * steps), (0, 0)))
    sent = sent.reshape(shards, own_rows, 3 * cols + 128)
    got = jnp.sum(exchange(sent).astype(jnp.float32), axis=0)
    inv_one = lax.rsqrt(jnp.sum(got[:, 3 * cols :], axis=1) / width_all + EPSILON)
    proj = got[:, : 3 * cols] * inv_one[:, None]
    own_len = lax.dynamic_slice_in_dim(jnp.pad(cache_len, (0, filler)), seq_index * share, share, 0)
    positions = (own_len[:, None] + jnp.arange(steps)[None, :]).reshape(own_rows)
    query = rotate(proj[:, :cols], positions, HEAD_DIM).astype(jnp.bfloat16)
    fresh_key = rotate(proj[:, cols : 2 * cols], positions, HEAD_DIM).astype(jnp.bfloat16)
    fresh_value = proj[:, 2 * cols :].astype(jnp.bfloat16)
    all_query = lax.all_gather(query, "seq", axis=0, tiled=True)[:row_count]
    all_query, fresh_pair = lax.optimization_barrier(
        (all_query, jnp.concatenate([fresh_key, fresh_value], axis=1))
    )
    all_pair = lax.all_gather(fresh_pair, "seq", axis=0, tiled=True)[:row_count]
    all_pair = all_pair.reshape(requests, steps, 2 * cols).transpose(1, 0, 2)

    needed = (cache_len + steps + page_size - 1) // page_size
    columns = jnp.arange(page_table.shape[1])
    in_use = columns[None, :] < needed[:, None]
    local_pages = page_table - seq_index * pages_loc
    page_hits = in_use[:, :, None] & (
        local_pages[:, :, None] == jnp.arange(pages_loc)[None, None, :]
    )
    owned_by = jnp.any(page_hits, axis=1)
    page_starts = jnp.sum(jnp.where(page_hits, columns[None, :, None] * page_size, 0), axis=(0, 1))
    page_len = jnp.sum(jnp.where(owned_by, cache_len[:, None], 0), axis=0)
    owner = jnp.sum(jnp.where(owned_by, jnp.arange(requests)[:, None], 0), axis=0)
    count = page_len - page_starts
    page_sums, page_peak, page_total = attend_pages(
        owner.astype(jnp.int32),
        count.astype(jnp.int32),
        all_query.reshape(requests, steps, cols),
        key_cache,
        value_cache,
    )
    mask = owned_by[:, :, None, None]
    req_peak = jnp.max(jnp.where(mask, page_peak[None], LOWEST), axis=1)
    back_peak = jnp.max(jnp.where(mask, req_peak[:, None], LOWEST), axis=0)
    factor = jnp.exp(page_peak - back_peak)
    factor = jnp.where((count > 0)[:, None, None] & jnp.any(owned_by, axis=0)[:, None, None], factor, 0.0)
    owner_float = owned_by.astype(jnp.float32)
    req_total = jnp.einsum(
        "rp,pnh->rnh", owner_float, page_total * factor, precision=lax.Precision.HIGHEST
    )
    scaled = page_sums * jnp.repeat(factor, HEAD_DIM, axis=2)
    req_sums = jnp.einsum("rp,pnc->rnc", owner_float, scaled, precision=lax.Precision.HIGHEST)
    extra = jnp.concatenate(pieces(req_peak, 3) + pieces(req_total, 3), axis=2)
    spare = -extra.shape[2] % 128
    extra = jnp.pad(extra, ((0, 0), (0, 0), (0, spare)))
    sent = jnp.concatenate([req_sums.astype(jnp.bfloat16), extra], axis=2)
    sent = jnp.pad(sent, ((0, filler), (0, 0), (0, 0)))
    got = exchange(sent.reshape(shards, own_rows, sent.shape[2])).astype(jnp.float32)
    sums = got[:, :, :cols]
    bits = got[:, :, cols : cols + 6 * heads].reshape(shards, own_rows, 6, heads)
    peaks = bits[:, :, 0] + bits[:, :, 1] + bits[:, :, 2]
    totals = bits[:, :, 3] + bits[:, :, 4] + bits[:, :, 5]
    q_own = query.astype(jnp.float32).reshape(share, steps, 1, heads, HEAD_DIM)
    k_own = fresh_key.astype(jnp.float32).reshape(share, 1, steps, heads, HEAD_DIM)
    v_own = fresh_value.astype(jnp.float32).reshape(share, 1, steps, cols)
    fresh_scores = jnp.sum(q_own * k_own, axis=4) * (HEAD_DIM ** (-0.5))
    seen = (jnp.arange(steps)[None, :] <= jnp.arange(steps)[:, None])[None, :, :, None]
    fresh_scores = jnp.where(seen, fresh_scores, LOWEST)
    best = jnp.maximum(
        jnp.max(peaks, axis=0).reshape(share, steps, heads), jnp.max(fresh_scores, axis=2)
    )
    fresh_weights = jnp.where(seen, jnp.exp(fresh_scores - best[:, :, None]), 0.0)
    scale = jnp.exp(peaks - best.reshape(1, own_rows, heads))
    denominator = jnp.sum(totals * scale, axis=0) + jnp.sum(fresh_weights, axis=2).reshape(
        own_rows, heads
    )
    lowered = lax.reduce_precision(fresh_weights, 8, 7)
    numerator = jnp.sum(sums * jnp.repeat(scale, HEAD_DIM, axis=2), axis=0) + jnp.sum(
        jnp.repeat(lowered, HEAD_DIM, axis=3) * v_own, axis=2
    ).reshape(own_rows, cols)
    attended = (numerator / jnp.repeat(denominator, HEAD_DIM, axis=1)).astype(jnp.bfloat16)
    all_attended = lax.all_gather(attended, "seq", axis=0, tiled=True)[:row_count]
    projected = col_scatter(jnp.dot(all_attended, w_out, preferred_element_type=jnp.float32))
    half = projected.shape[0]
    wide_half = lax.dynamic_slice_in_dim(wide_in, lax.axis_index("col") * half, half, 0)
    residual = (wide_half + projected).astype(jnp.bfloat16)
    flat_rows = col_gather(lax.all_gather(residual, "seq", axis=1, tiled=True))

    chosen = route_ids.transpose(1, 0, 2).reshape(row_count, 2)
    expert_ids = jnp.arange(expert_count)
    w_pair = w_gate_up.reshape(experts_loc, width_all, 2 * ff_loc)
    pair_sum = jnp.einsum("rc,ecf->ref", flat_rows, w_pair, preferred_element_type=jnp.float32)
    wide_rows = flat_rows.astype(jnp.float32)
    square_sum = jnp.sum(wide_rows * wide_rows, axis=1)
    router_sum = jnp.dot(flat_rows, w_router, preferred_element_type=jnp.float32)
    inv_two = lax.rsqrt(square_sum / width_all + EPSILON)
    logits = router_sum * inv_two[:, None]
    first_pick = chosen[:, 0:1] == expert_ids[None, :]
    second_pick = chosen[:, 1:2] == expert_ids[None, :]
    first_share = jax.nn.sigmoid(
        jnp.sum(jnp.where(first_pick, logits, 0.0), axis=1)
        - jnp.sum(jnp.where(second_pick, logits, 0.0), axis=1)
    )
    gate_rows = jnp.where(first_pick, first_share[:, None], 0.0) + jnp.where(
        second_pick, 1.0 - first_share[:, None], 0.0
    )
    gate_local = lax.dynamic_slice_in_dim(gate_rows, expert_base, experts_loc, 1)
    pair_sum = pair_sum * inv_two[:, None, None]
    active = (jax.nn.silu(pair_sum[..., :ff_loc]) * pair_sum[..., ff_loc:]).astype(jnp.bfloat16)
    outputs = jnp.einsum("ref,efd->red", active, w_down, preferred_element_type=jnp.float32)
    weighted = jnp.sum(outputs * gate_local[:, :, None], axis=1)
    joined = col_scatter(weighted).astype(jnp.bfloat16)
    blocks = joined.reshape(half, shards, width_loc).transpose(1, 0, 2)
    mixture = jnp.sum(exchange(blocks).astype(jnp.float32), axis=0)
    layer_half = (residual.astype(jnp.float32) + mixture).astype(jnp.bfloat16)
    layer_rows = col_gather(layer_half).reshape(requests, steps, width_loc).transpose(1, 0, 2)
    return (layer_rows, all_pair[:, :, :cols], all_pair[:, :, cols:])


def solution(mesh):
    placed = (
        P(None, None, "seq"),
        P("seq", None, "col"),
        P("seq", None, "col"),
        P(),
        P(),
        P(),
        P(),
        P("seq", None, "col"),
        P("col", "seq"),
        P(),
        P("col", None, None, "seq"),
        P("col", "seq", None),
    )
    return jax.shard_map(
        local,
        mesh=mesh,
        in_specs=placed,
        out_specs=(P(None, None, "seq"), P(None, None, "col"), P(None, None, "col")),
        check_vma=False,
    )
```
